32 devices in a mesh: row: 4 (over z), col: 8 (over y, x, core).
Axes of the slice: x: 2, y: 2, z: 4, core: 2. Of those that a mesh axis runs over, the one named last changes fastest.
Arguments:
- factor: float32 [4, 1024, 4096], P(None, 'row', 'col'), may hold values from -0.125 to 0.125
- panel_inverse: float32 [4, 1024, 1024], P(None, 'row', 'col')
- sim_maps: float32 [4, 1024, 128], P(None, 'row'), may hold values from -6 to 6
- harmonics: bfloat16 [28000, 4096], P('col', 'row'), may hold values from -0.09375 to 0.09375
Outputs:
- solved: float32 [4, 1024, 128], P(None, 'row')
- projected: float32 [128, 28000], P('row', 'col')
The draws below stay inside these ranges and needn't reach their ends.
All inputs are finite; a program needn't handle non-finite values.
Results may differ from the reference program's by a relative error of at most 0.0029.
Values sent between devices are 32-bit elements; how exact they have to be, the bound alone decides.
A program may use at most 64 MiB of HBM per device.

```python
import math
import jax
import jax.numpy as jnp
from jax import lax

P_SIZE = 1024
PANELS = 4
MAPS = 128
MODES = 28000
ROWS = 4096


def draw_panel_inverse(key, part):
    first, second = jax.random.split(jax.random.fold_in(key, 17), 2)
    diagonal = jax.random.uniform(first, (PANELS, P_SIZE), jnp.float32, 1.0, 2.0)
    offdiag = jnp.clip(jax.random.normal(second, (PANELS, P_SIZE, P_SIZE), jnp.float32), -4.0, 4.0) * (0.5 / math.sqrt(P_SIZE))
    unit = jnp.eye(P_SIZE, dtype=jnp.float32)
    matrix = offdiag * (1.0 - unit) + unit * diagonal[:, :, None]
    return matrix


def steps_of(stream_key, extent, pieces, low, top_value):
    def one(axis_at, parts):
        steps = jax.random.uniform(jax.random.fold_in(jax.random.fold_in(stream_key, 6), axis_at), (parts,), jnp.float32, low / len(pieces), top_value / len(pieces))
        return jnp.repeat(jnp.exp(steps), extent[axis_at] // parts).reshape((-1,) + (1,) * (len(extent) - axis_at - 1))

    gain = one(*pieces[0])
    for cut in pieces[1:]:
        gain = gain * one(*cut)
    return gain


def scatter_about(rng, dims, deviation, reach, pieces=(), kind=jnp.bfloat16):
    drawn = jax.random.normal(rng, dims, jnp.float32) * deviation
    if len(pieces) > 0:
        drawn = steps_of(rng, dims, pieces, -0.22, 0.18) * drawn
    return jnp.clip(drawn, min=-reach, max=reach).astype(kind)


def setup_inputs(seed: int = 0) -> dict:
    streams_of = jax.random.split(jax.random.key(seed), 5)
    return {
        "factor": scatter_about(streams_of[0], (PANELS, P_SIZE, P_SIZE * PANELS), (2 * P_SIZE) ** -0.5, 0.125, ((1, 4), (2, 8)), jnp.float32),
        "panel_inverse": draw_panel_inverse(jax.random.fold_in(streams_of[4], 71), 0),
        "sim_maps": scatter_about(streams_of[2], (PANELS, P_SIZE, MAPS), 1.0, 6.0, ((1, 4),), jnp.float32),
        "harmonics": scatter_about(streams_of[3], (MODES, P_SIZE * PANELS), ROWS ** -0.5, 0.09375, ((0, 8), (1, 4))),
    }


def reference(factor, panel_inverse, sim_maps, harmonics):
    blocks = jnp.transpose(factor.reshape(PANELS, P_SIZE, P_SIZE, PANELS), (0, 1, 3, 2))
    solved = jnp.zeros((PANELS, P_SIZE, MAPS), jnp.float32)
    for panel in range(PANELS):
        update = jnp.einsum("ajb,jbm->am", blocks[panel], solved, precision=lax.Precision.HIGHEST)
        rhs_now = sim_maps[panel] - update
        result = jnp.dot(panel_inverse[panel], rhs_now, precision=lax.Precision.HIGHEST, preferred_element_type=jnp.float32)
        solved = solved.at[panel].set(result)
    solved_low = solved.astype(jnp.bfloat16)
    stacked = jnp.transpose(solved_low, (1, 0, 2)).reshape(P_SIZE * PANELS, MAPS)
    coeffs = jnp.dot(harmonics.astype(jnp.float32), stacked.astype(jnp.float32), precision=lax.Precision.HIGHEST, preferred_element_type=jnp.float32)
    return solved, jnp.transpose(coeffs)
```

```python
import functools

import jax
import jax.numpy as jnp
from jax import lax
from jax.experimental import pallas as pl
from jax.experimental.pallas import tpu as pltpu
from jax.sharding import PartitionSpec as P

MESH = pl.DeviceIdType.MESH
CHUNK = 512
LANES = 128
SUBLANES = 8


def split(value):
    high = value.astype(jnp.bfloat16)
    low = (value - high.astype(jnp.float32)).astype(jnp.bfloat16)
    return high, low


def dot3(mat_high, mat_low, value):
    high, low = split(value)
    mul = functools.partial(jnp.dot, preferred_element_type=jnp.float32)
    return mul(mat_high, high) + (mul(mat_high, low) + mul(mat_low, high))


def kernel(
    n_row, n_col, factor_hbm, inv_hbm, sim_hbm, harm_hbm, solved_ref, proj_ref,
    factor, inv, sim, harm, f_high, f_low, i_high, i_low,
    partial, gathered, piece, xbuf, xint, sol, stacked, outs, landed,
    load_sem, rs_send, rs_recv, bc_send, bc_recv, ag_send, ag_recv, pj_send, pj_recv,
):
    panels, rows, maps = sim.shape
    cols = inv.shape[2]
    part = rows // n_col
    out_rows = maps // n_row
    stages = 2 * panels - 1
    modes = harm.shape[0]
    chunks = outs.shape[0]
    r, c = lax.axis_index("row"), lax.axis_index("col")
    me = r * n_col + c
    total = n_row * n_col

    loads = [
        pltpu.make_async_copy(src, dst, load_sem.at[i])
        for i, (src, dst) in enumerate(
            ((sim_hbm, sim), (inv_hbm, inv), (factor_hbm, factor), (harm_hbm, harm))
        )
    ]
    for load in loads:
        load.start()

    barrier = pltpu.get_barrier_semaphore()

    def greet(d, carry):
        peer = (me + d) % total
        pl.semaphore_signal(
            barrier, inc=1, device_id=(peer // n_col, peer % n_col), device_id_type=MESH
        )
        return carry

    lax.fori_loop(1, total, greet, 0)
    xint[...] = jnp.zeros_like(xint)
    loads[0].wait()
    loads[1].wait()
    for k in range(panels):
        i_high[k], i_low[k] = split(inv[k])
    pl.semaphore_wait(barrier, total - 1)

    mine = pl.ds(pl.multiple_of(c * part, part), part)
    owner = (r * rows + c * part) // cols
    inside = (r * rows + c * part) % cols
    place = pl.ds(pl.multiple_of(inside, part), part)
    pieces = cols // part

    def spread(stage, source):
        def one(d, carry):
            pltpu.make_async_remote_copy(
                src_ref=source,
                dst_ref=xbuf.at[stage, place],
                send_sem=bc_send.at[stage],
                recv_sem=bc_recv.at[stage],
                device_id=((r + d) % n_row, owner),
                device_id_type=MESH,
            ).start()
            return carry

        @pl.when(owner != c)
        def _():
            one(0, 0)

        @pl.when(owner == c)
        def _():
            xbuf[stage, place] = source[...]

        lax.fori_loop(1, n_row, one, 0)

    def drain(sem, ref):
        pltpu.make_async_copy(ref, ref, sem).wait()

    def take(stage):
        @pl.when(owner != c)
        def _():
            drain(bc_recv.at[stage], xbuf.at[stage])

        @pl.when(owner == c)
        def _():
            drain(bc_recv.at[stage], xbuf.at[stage, pl.ds(0, (pieces - 1) * part)])

    def reduce(stage, value):
        partial[stage] = value

        def one(d, carry):
            peer = (c + d) % n_col
            pltpu.make_async_remote_copy(
                src_ref=partial.at[stage, pl.ds(pl.multiple_of(peer * part, part), part)],
                dst_ref=gathered.at[stage, d - 1],
                send_sem=rs_send.at[stage],
                recv_sem=rs_recv.at[stage],
                device_id=(r, peer),
                device_id_type=MESH,
            ).start()
            return carry

        lax.fori_loop(1, n_col, one, 0)
        return

    def reduced(stage):
        drain(rs_recv.at[stage], gathered.at[stage])
        total_value = partial[stage, mine]
        for d in range(n_col - 1):
            total_value = total_value + gathered[stage, d]
        return total_value

    spread(0, sim.at[0, mine])
    for stage in range(stages):
        take(stage)
        if stage % 2 == 0:
            k = stage // 2
            reduce(stage, dot3(i_high[k], i_low[k], xbuf[stage]))
            if stage == 0:
                loads[2].wait()
                for j in range(1, panels):
                    f_high[j - 1], f_low[j - 1] = split(factor[j])
            piece[stage] = reduced(stage)
            if stage + 1 < stages:
                spread(stage + 1, piece.at[stage])

            def share(d, carry):
                peer = (c + d) % n_col
                pltpu.make_async_remote_copy(
                    src_ref=piece.at[stage],
                    dst_ref=sol.at[k, mine],
                    send_sem=ag_send.at[k],
                    recv_sem=ag_recv.at[k],
                    device_id=(r, peer),
                    device_id_type=MESH,
                ).start()
                return carry

            lax.fori_loop(1, n_col, share, 0)
            sol[k, mine] = piece[stage]
        else:
            k = (stage + 1) // 2
            xint[pl.ds(k - 1, cols, stride=panels), :] = xbuf[stage]
            reduce(stage, dot3(f_high[k - 1], f_low[k - 1], xint[...]))
            piece[stage] = sim[k, mine] - reduced(stage)
            spread(stage + 1, piece.at[stage])

    rest = pl.ds(0, rows - part)
    loads[3].wait()
    for k in range(panels):
        drain(ag_recv.at[k], sol.at[k, rest])
        value = sol[k]
        solved_ref[k] = value
        stacked[pl.ds(k, rows, stride=panels), :] = value
    turned = jnp.transpose(stacked[...], (1, 0)).astype(jnp.bfloat16)
    for i in range(chunks):
        size = min(CHUNK, modes - i * CHUNK)
        outs[i, :, :size] = lax.dot_general(
            turned, harm[i * CHUNK : i * CHUNK + size, :],
            (((1,), (1,)), ((), ())), preferred_element_type=jnp.float32,
        )

        def send(d, carry):
            peer = (r + d) % n_row
            pltpu.make_async_remote_copy(
                src_ref=outs.at[i, pl.ds(pl.multiple_of(peer * out_rows, out_rows), out_rows)],
                dst_ref=landed.at[i, d - 1],
                send_sem=pj_send.at[i],
                recv_sem=pj_recv.at[i],
                device_id=(peer, c),
                device_id_type=MESH,
            ).start()
            return carry

        lax.fori_loop(1, n_row, send, 0)

    own = pl.ds(pl.multiple_of(r * out_rows, out_rows), out_rows)
    for i in range(chunks):
        size = min(CHUNK, modes - i * CHUNK)
        drain(pj_recv.at[i], landed.at[i])
        value = outs[i, own]
        for d in range(n_row - 1):
            value = value + landed[i, d]
        proj_ref[:, i * CHUNK : i * CHUNK + size] = value[:, :size]

    for stage in range(stages):
        drain(rs_send.at[stage], gathered.at[stage])

        @pl.when(owner != c)
        def _():
            drain(bc_send.at[stage], sol.at[0, pl.ds(0, n_row * part)])

        @pl.when(owner == c)
        def _():
            drain(bc_send.at[stage], sol.at[0, pl.ds(0, (n_row - 1) * part)])

    for k in range(panels):
        drain(ag_send.at[k], sol.at[k, rest])
    for i in range(chunks):
        drain(pj_send.at[i], landed.at[i])


def fused(n_row, n_col, factor, inv, sim, harm):
    panels, rows, maps = sim.shape
    cols = inv.shape[2]
    modes = harm.shape[0]
    part = rows // n_col
    stages = 2 * panels - 1
    chunks = -(-modes // CHUNK)
    f32, bf16 = jnp.float32, jnp.bfloat16
    any_space = pl.BlockSpec(memory_space=pl.ANY)
    vmem = pl.BlockSpec(memory_space=pltpu.VMEM)
    dma = pltpu.SemaphoreType.DMA
    return pl.pallas_call(
        functools.partial(kernel, n_row, n_col),
        out_shape=(
            jax.ShapeDtypeStruct(sim.shape, f32),
            jax.ShapeDtypeStruct((maps // n_row, modes), f32),
        ),
        in_specs=[any_space] * 4,
        out_specs=(vmem, vmem),
        scratch_shapes=[
            pltpu.VMEM(factor.shape, f32),
            pltpu.VMEM(inv.shape, f32),
            pltpu.VMEM(sim.shape, f32),
            pltpu.VMEM(harm.shape, bf16),
            pltpu.VMEM((panels - 1,) + factor.shape[1:], bf16),
            pltpu.VMEM((panels - 1,) + factor.shape[1:], bf16),
            pltpu.VMEM(inv.shape, bf16),
            pltpu.VMEM(inv.shape, bf16),
            pltpu.VMEM((stages, rows, maps), f32),
            pltpu.VMEM((stages, n_col - 1, part, maps), f32),
            pltpu.VMEM((stages, part, maps), f32),
            pltpu.VMEM((stages, cols, maps), f32),
            pltpu.VMEM((cols * panels, maps), f32),
            pltpu.VMEM(sim.shape, f32),
            pltpu.VMEM((rows * panels, maps), f32),
            pltpu.VMEM((chunks, maps, CHUNK), f32),
            pltpu.VMEM((chunks, n_row - 1, maps // n_row, CHUNK), f32),
            dma((4,)),
            dma((stages,)), dma((stages,)), dma((stages,)), dma((stages,)),
            dma((panels,)), dma((panels,)),
            dma((chunks,)), dma((chunks,)),
        ],
        compiler_params=pltpu.CompilerParams(
            collective_id=0, has_side_effects=True, vmem_limit_bytes=48 * 1024 * 1024
        ),
    )(factor, inv, sim, harm)


def plain(factor, panel_inverse, sim_maps, harmonics):
    panels = factor.shape[0]
    row_count = factor.shape[1]
    col_count = factor.shape[2] // panels
    map_count = sim_maps.shape[2]
    col_index = lax.axis_index("col")
    columns = jnp.zeros((col_count, panels, map_count), jnp.float32)
    results = []
    for panel in range(panels):
        flat_cols = columns.reshape(col_count * panels, map_count)
        partial_value = jnp.dot(
            factor[panel], flat_cols,
            precision=lax.Precision.HIGHEST, preferred_element_type=jnp.float32,
        )
        update = lax.psum(partial_value, "col")
        rhs_now = sim_maps[panel] - update
        whole = lax.all_gather(rhs_now, "row", axis=0, tiled=True)
        piece = lax.dynamic_slice_in_dim(whole, col_index * col_count, col_count, 0)
        partial_inv = jnp.dot(
            panel_inverse[panel], piece,
            precision=lax.Precision.HIGHEST, preferred_element_type=jnp.float32,
        )
        result = lax.psum(partial_inv, "col")
        whole_solved = lax.all_gather(result, "row", axis=0, tiled=True)
        solved_piece = lax.dynamic_slice_in_dim(whole_solved, col_index * col_count, col_count, 0)
        columns = columns.at[:, panel, :].set(solved_piece)
        results.append(result)
    solved = jnp.stack(results)
    solved_low = solved.astype(jnp.bfloat16)
    stacked = jnp.transpose(solved_low, (1, 0, 2)).reshape(row_count * panels, map_count)
    projected = lax.psum_scatter(
        lax.dot_general(
            stacked, harmonics, (((0,), (1,)), ((), ())), preferred_element_type=jnp.float32
        ),
        "row", scatter_dimension=0, tiled=True,
    )
    return (solved, projected)


def solution(mesh):
    n_row, n_col = mesh.shape["row"], mesh.shape["col"]

    def local(factor, panel_inverse, sim_maps, harmonics):
        _, rows, maps = sim_maps.shape
        cols = panel_inverse.shape[2]
        part = rows // n_col
        fits = (
            rows % n_col == 0
            and part % SUBLANES == 0
            and cols % part == 0
            and cols % LANES == 0
            and maps % LANES == 0
            and maps // n_row % SUBLANES == 0
            and rows % cols == 0
        )
        if not fits:
            return plain(factor, panel_inverse, sim_maps, harmonics)
        return fused(n_row, n_col, factor, panel_inverse, sim_maps, harmonics)

    in_specs = (P(None, "row", "col"), P(None, "row", "col"), P(None, "row", None), P("col", "row"))
    out_specs = (P(None, "row", None), P("row", "col"))
    return jax.shard_map(local, mesh=mesh, in_specs=in_specs, out_specs=out_specs, check_vma=False)
```

```python
import functools

import jax
import jax.numpy as jnp
from jax import lax
from jax.experimental import pallas as pl
from jax.experimental.pallas import tpu as pltpu
from jax.sharding import PartitionSpec as P

MESH = pl.DeviceIdType.MESH
CHUNK = 896
LANES = 128
SUBLANES = 8


def split(value):
    high = value.astype(jnp.bfloat16)
    low = (value - high.astype(jnp.float32)).astype(jnp.bfloat16)
    return high, low


def dot3(mat_high, mat_low, value):
    high, low = split(value)
    mul = functools.partial(jnp.dot, preferred_element_type=jnp.float32)
    return mul(mat_high, high) + (mul(mat_high, low) + mul(mat_low, high))


def kernel(
    n_row, n_col, factor_hbm, inv_hbm, sim_hbm, harm_hbm, solved_ref, proj_ref,
    factor, inv, sim, harm, f_high, f_low, i_high, i_low,
    partial, gathered, piece, xbuf, xint, ibuf, fcol, fbuf, g_high, g_low, sol, stacked, outs, up, down,
    load_sem, rs_send, rs_recv, bc_send, bc_recv, im_send, im_recv, ia_send, ia_recv, fz_send, fz_recv,
    ag_send, ag_recv, pj_send, up_sem, down_sem,
):
    panels, rows, maps = sim.shape
    cols = inv.shape[2]
    part = rows // n_col
    out_rows = maps // n_row
    stages = 2 * panels - 1
    modes = harm.shape[0]
    chunks = outs.shape[0]
    r, c = lax.axis_index("row"), lax.axis_index("col")
    me = r * n_col + c
    total = n_row * n_col

    loads = [
        pltpu.make_async_copy(src, dst, load_sem.at[i])
        for i, (src, dst) in enumerate(
            ((sim_hbm, sim), (inv_hbm, inv), (factor_hbm, factor), (harm_hbm, harm))
        )
    ]
    for load in loads:
        load.start()

    barrier = pltpu.get_barrier_semaphore()

    def greet(d, carry):
        peer = (me + d) % total
        pl.semaphore_signal(
            barrier, inc=1, device_id=(peer // n_col, peer % n_col), device_id_type=MESH
        )
        return carry

    lax.fori_loop(1, total, greet, 0)
    xint[...] = jnp.zeros_like(xint)
    loads[0].wait()
    loads[1].wait()
    for k in range(panels):
        i_high[k], i_low[k] = split(inv[k])
    pl.semaphore_wait(barrier, total - 1)

    mine = pl.ds(pl.multiple_of(c * part, part), part)
    owner = (r * rows + c * part) // cols
    inside = (r * rows + c * part) % cols
    place = pl.ds(pl.multiple_of(inside, part), part)
    pieces = cols // part

    def spread(stage, source):
        def one(d, carry):
            pltpu.make_async_remote_copy(
                src_ref=source,
                dst_ref=xbuf.at[stage, place],
                send_sem=bc_send.at[stage],
                recv_sem=bc_recv.at[stage],
                device_id=((r + d) % n_row, owner),
                device_id_type=MESH,
            ).start()
            return carry

        @pl.when(owner != c)
        def _():
            one(0, 0)

        @pl.when(owner == c)
        def _():
            xbuf[stage, place] = source[...]

        lax.fori_loop(1, n_row, one, 0)

    def drain(sem, ref):
        pltpu.make_async_copy(ref, ref, sem).wait()

    def take(stage):
        @pl.when(owner != c)
        def _():
            drain(bc_recv.at[stage], xbuf.at[stage])

        @pl.when(owner == c)
        def _():
            drain(bc_recv.at[stage], xbuf.at[stage, pl.ds(0, (pieces - 1) * part)])

    def reduce(stage, value):
        partial[stage] = value

        def one(d, carry):
            peer = (c + d) % n_col
            pltpu.make_async_remote_copy(
                src_ref=partial.at[stage, pl.ds(pl.multiple_of(peer * part, part), part)],
                dst_ref=gathered.at[stage, d - 1],
                send_sem=rs_send.at[stage],
                recv_sem=rs_recv.at[stage],
                device_id=(r, peer),
                device_id_type=MESH,
            ).start()
            return carry

        lax.fori_loop(1, n_col, one, 0)
        return

    def reduced(stage):
        drain(rs_recv.at[stage], gathered.at[stage])
        total_value = partial[stage, mine]
        for d in range(n_col - 1):
            total_value = total_value + gathered[stage, d]
        return total_value

    def share(k, source):
        def one(d, carry):
            pltpu.make_async_remote_copy(
                src_ref=source,
                dst_ref=sol.at[k, mine],
                send_sem=ag_send.at[k],
                recv_sem=ag_recv.at[k],
                device_id=(r, (c + d) % n_col),
                device_id_type=MESH,
            ).start()
            return carry

        lax.fori_loop(1, n_col, one, 0)
        sol[k, mine] = source[...]

    mate = c + 1 - 2 * (c % 2)

    def own_block(g):
        ibuf[g, c] = inv[g + 2]
        pltpu.make_async_remote_copy(
            src_ref=inv.at[g + 2], dst_ref=ibuf.at[g, c],
            send_sem=im_send.at[g, 0], recv_sem=im_recv.at[g],
            device_id=(r, mate), device_id_type=MESH,
        ).start()

    def across(g, d):
        pltpu.make_async_remote_copy(
            src_ref=inv.at[g + 2], dst_ref=ibuf.at[g, c],
            send_sem=ia_send.at[g, d - 1], recv_sem=ia_recv.at[g, d - 1],
            device_id=(r, (c + 2 * d) % n_col), device_id_type=MESH,
        ).start()

    def relay(g, d):
        source = (c + n_col - 2 * d) % n_col
        drain(ia_recv.at[g, d - 1], ibuf.at[g, source])
        pltpu.make_async_remote_copy(
            src_ref=ibuf.at[g, source], dst_ref=ibuf.at[g, source],
            send_sem=im_send.at[g, d], recv_sem=im_recv.at[g],
            device_id=(r, mate), device_id_type=MESH,
        ).start()

    def along(g, d):
        pltpu.make_async_remote_copy(
            src_ref=fcol.at[g], dst_ref=fbuf.at[g, r],
            send_sem=fz_send.at[g], recv_sem=fz_recv.at[g],
            device_id=((r + d) % n_row, c), device_id_type=MESH,
        ).start()

    def pick(g):
        wide, narrow = cols * panels, cols
        at = lax.broadcasted_iota(jnp.int32, (wide, narrow), 0)
        to = lax.broadcasted_iota(jnp.int32, (wide, narrow), 1)
        chosen = jnp.where(at == to * panels + (g + 1), 1.0, 0.0).astype(jnp.bfloat16)
        mul = functools.partial(jnp.dot, preferred_element_type=jnp.float32)
        fcol[g] = mul(f_high[g + 1], chosen) + mul(f_low[g + 1], chosen)
        fbuf[g, r] = fcol[g]

    def product(g):
        drain(im_recv.at[g], ibuf.at[g, pl.ds(0, n_col // 2)])
        drain(fz_recv.at[g], fbuf.at[g, pl.ds(0, n_row - 1)])
        value = jnp.zeros((rows, cols), jnp.float32)
        per = rows // cols
        for q in range(n_col):
            high, low = split(ibuf[g, q])
            value = value + dot3(high, low, fbuf[g, q // per, (q % per) * cols : (q % per + 1) * cols])
        g_high[g], g_low[g] = split(value)

    half = n_col // 2
    plan = {}
    for g in range(panels - 2):
        at = 1 + 3 * g
        tasks = [(0, own_block, (g,))]
        tasks += [(d - 1, across, (g, d)) for d in range(1, half)]
        tasks += [(min(d - 1, 2), along, (g, d)) for d in range(1, n_row)]
        tasks += [(3, relay, (g, d)) for d in range(1, half)]
        tasks += [(4, product, (g,))]
        for offset, task, arguments in tasks:
            plan.setdefault(at + offset, []).append((task, arguments))

    def aside(point):
        for task, arguments in plan.pop(point, ()):
            task(*arguments)

    def extra(k):
        return panels + k - 1

    spread(0, sim.at[0, mine])
    loads[2].wait()
    for j in range(1, panels):
        f_high[j - 1], f_low[j - 1] = split(factor[j])
    for g in range(panels - 2):
        pick(g)
    take(0)
    reduce(0, dot3(i_high[0], i_low[0], xbuf[0]))
    aside(1)
    piece[0] = reduced(0)
    spread(1, piece.at[0])
    aside(2)
    share(0, piece.at[0])
    take(1)
    xint[pl.ds(0, cols, stride=panels), :] = xbuf[1]
    reduce(1, dot3(f_high[0], f_low[0], xint[...]))
    if panels > 2:
        reduce(extra(2), dot3(f_high[1], f_low[1], xint[...]))
    aside(3)
    piece[1] = sim[1, mine] - reduced(1)
    spread(2, piece.at[1])
    if panels > 2:
        piece[extra(2)] = sim[2, mine] - reduced(extra(2))
        spread(extra(2), piece.at[extra(2)])
    aside(4)
    take(2)
    reduce(2, dot3(i_high[1], i_low[1], xbuf[2]))
    aside(5)
    piece[2] = reduced(2)
    point = 6
    for k in range(2, panels):
        slot = k + 1
        spread(slot, piece.at[slot - 1])
        if k > 2:
            piece[extra(k)] = sim[k, mine] - reduced(extra(k))
            spread(extra(k), piece.at[extra(k)])
        share(k - 1, piece.at[slot - 1])
        aside(point)
        take(extra(k))
        ahead = dot3(i_high[k], i_low[k], xbuf[extra(k)])
        take(slot)
        reduce(slot, ahead - dot3(g_high[k - 2], g_low[k - 2], xbuf[slot]))
        if k + 1 < panels:
            xint[pl.ds(k - 1, cols, stride=panels), :] = xbuf[slot]
            reduce(extra(k + 1), dot3(f_high[k], f_low[k], xint[...]))
        aside(point + 1)
        piece[slot] = reduced(slot)
        point = point + 2
    share(panels - 1, piece.at[panels])
    assert not plan

    rest = pl.ds(0, rows - part)
    loads[3].wait()
    for k in range(panels):
        drain(ag_recv.at[k], sol.at[k, rest])
        value = sol[k]
        solved_ref[k] = value
        stacked[pl.ds(k, rows, stride=panels), :] = value
    turned = jnp.transpose(stacked[...], (1, 0)).astype(jnp.bfloat16)

    def forward(i, p, step, slots, sems):
        block = pl.ds(p * out_rows, out_rows)

        @pl.when((r - step >= 0) & (r - step < n_row))
        def _():
            drain(sems.at[i, p], slots.at[i, p])
            outs[i, block] = outs[i, block] + slots[i, p]

        pltpu.make_async_remote_copy(
            src_ref=outs.at[i, block],
            dst_ref=slots.at[i, p],
            send_sem=pj_send.at[i, p],
            recv_sem=sems.at[i, p],
            device_id=(r + step, c),
            device_id_type=MESH,
        ).start()

    own = pl.ds(pl.multiple_of(r * out_rows, out_rows), out_rows)
    for i in range(chunks + n_row - 1):
        if i < chunks:
            size = min(CHUNK, modes - i * CHUNK)
            outs[i, :, :size] = lax.dot_general(
                turned, harm[i * CHUNK : i * CHUNK + size, :],
                (((1,), (1,)), ((), ())), preferred_element_type=jnp.float32,
            )
        for step, lag, slots, sems in ((1, r, up, up_sem), (-1, n_row - 1 - r, down, down_sem)):
            at = i - lag
            for p in range(n_row):
                target = n_row - 1 - p if step == 1 else p

                @pl.when(((target - r) * step > 0) & (at >= 0) & (at < chunks))
                def _():
                    forward(at, target, step, slots, sems)

    for i in range(chunks):
        size = min(CHUNK, modes - i * CHUNK)

        @pl.when(r > 0)
        def _():
            drain(up_sem.at[i, r], up.at[i, r])
            outs[i, own] = outs[i, own] + up[i, r]

        @pl.when(r < n_row - 1)
        def _():
            drain(down_sem.at[i, r], down.at[i, r])
            outs[i, own] = outs[i, own] + down[i, r]

        proj_ref[:, i * CHUNK : i * CHUNK + size] = outs[i, own][:, :size]

    for stage in range(stages):
        drain(rs_send.at[stage], gathered.at[stage])

        @pl.when(owner != c)
        def _():
            drain(bc_send.at[stage], sol.at[0, pl.ds(0, n_row * part)])

        @pl.when(owner == c)
        def _():
            drain(bc_send.at[stage], sol.at[0, pl.ds(0, (n_row - 1) * part)])

    for g in range(panels - 2):
        for d in range(half):
            drain(im_send.at[g, d], ibuf.at[g, d])
        for d in range(half - 1):
            drain(ia_send.at[g, d], ibuf.at[g, d])
        drain(fz_send.at[g], fbuf.at[g, pl.ds(0, n_row - 1)])
    for k in range(panels):
        drain(ag_send.at[k], sol.at[k, rest])

    for i in range(chunks):
        for p in range(n_row):
            @pl.when(r != p)
            def _():
                drain(pj_send.at[i, p], up.at[i, p])


def fused(n_row, n_col, factor, inv, sim, harm):
    panels, rows, maps = sim.shape
    cols = inv.shape[2]
    modes = harm.shape[0]
    part = rows // n_col
    stages = 2 * panels - 1
    chunks = -(-modes // CHUNK)
    f32, bf16 = jnp.float32, jnp.bfloat16
    any_space = pl.BlockSpec(memory_space=pl.ANY)
    vmem = pl.BlockSpec(memory_space=pltpu.VMEM)
    dma = pltpu.SemaphoreType.DMA
    return pl.pallas_call(
        functools.partial(kernel, n_row, n_col),
        out_shape=(
            jax.ShapeDtypeStruct(sim.shape, f32),
            jax.ShapeDtypeStruct((maps // n_row, modes), f32),
        ),
        in_specs=[any_space] * 4,
        out_specs=(vmem, vmem),
        scratch_shapes=[
            pltpu.VMEM(factor.shape, f32),
            pltpu.VMEM(inv.shape, f32),
            pltpu.VMEM(sim.shape, f32),
            pltpu.VMEM(harm.shape, bf16),
            pltpu.VMEM((panels - 1,) + factor.shape[1:], bf16),
            pltpu.VMEM((panels - 1,) + factor.shape[1:], bf16),
            pltpu.VMEM(inv.shape, bf16),
            pltpu.VMEM(inv.shape, bf16),
            pltpu.VMEM((stages, rows, maps), f32),
            pltpu.VMEM((stages, n_col - 1, part, maps), f32),
            pltpu.VMEM((stages, part, maps), f32),
            pltpu.VMEM((stages, cols, maps), f32),
            pltpu.VMEM((cols * panels, maps), f32),
            pltpu.VMEM((panels - 2, n_col, rows, cols), f32),
            pltpu.VMEM((panels - 2, rows, cols), f32),
            pltpu.VMEM((panels - 2, n_row, rows, cols), f32),
            pltpu.VMEM((panels - 2, rows, cols), bf16),
            pltpu.VMEM((panels - 2, rows, cols), bf16),
            pltpu.VMEM(sim.shape, f32),
            pltpu.VMEM((rows * panels, maps), f32),
            pltpu.VMEM((chunks, maps, CHUNK), f32),
            pltpu.VMEM((chunks, n_row, maps // n_row, CHUNK), f32),
            pltpu.VMEM((chunks, n_row, maps // n_row, CHUNK), f32),
            dma((4,)),
            dma((stages,)), dma((stages,)), dma((stages,)), dma((stages,)),
            dma((panels - 2, n_col // 2)), dma((panels - 2,)),
            dma((panels - 2, n_col // 2 - 1)), dma((panels - 2, n_col // 2 - 1)),
            dma((panels - 2,)), dma((panels - 2,)),
            dma((panels,)), dma((panels,)),
            dma((chunks, n_row)), dma((chunks, n_row)), dma((chunks, n_row)),
        ],
        compiler_params=pltpu.CompilerParams(
            collective_id=0, has_side_effects=True, vmem_limit_bytes=62 * 1024 * 1024
        ),
    )(factor, inv, sim, harm)


def plain(factor, panel_inverse, sim_maps, harmonics):
    panels = factor.shape[0]
    row_count = factor.shape[1]
    col_count = factor.shape[2] // panels
    map_count = sim_maps.shape[2]
    col_index = lax.axis_index("col")
    columns = jnp.zeros((col_count, panels, map_count), jnp.float32)
    results = []
    for panel in range(panels):
        flat_cols = columns.reshape(col_count * panels, map_count)
        partial_value = jnp.dot(
            factor[panel], flat_cols,
            precision=lax.Precision.HIGHEST, preferred_element_type=jnp.float32,
        )
        update = lax.psum(partial_value, "col")
        rhs_now = sim_maps[panel] - update
        whole = lax.all_gather(rhs_now, "row", axis=0, tiled=True)
        piece = lax.dynamic_slice_in_dim(whole, col_index * col_count, col_count, 0)
        partial_inv = jnp.dot(
            panel_inverse[panel], piece,
            precision=lax.Precision.HIGHEST, preferred_element_type=jnp.float32,
        )
        result = lax.psum(partial_inv, "col")
        whole_solved = lax.all_gather(result, "row", axis=0, tiled=True)
        solved_piece = lax.dynamic_slice_in_dim(whole_solved, col_index * col_count, col_count, 0)
        columns = columns.at[:, panel, :].set(solved_piece)
        results.append(result)
    solved = jnp.stack(results)
    solved_low = solved.astype(jnp.bfloat16)
    stacked = jnp.transpose(solved_low, (1, 0, 2)).reshape(row_count * panels, map_count)
    projected = lax.psum_scatter(
        lax.dot_general(
            stacked, harmonics, (((0,), (1,)), ((), ())), preferred_element_type=jnp.float32
        ),
        "row", scatter_dimension=0, tiled=True,
    )
    return (solved, projected)


def solution(mesh):
    n_row, n_col = mesh.shape["row"], mesh.shape["col"]

    def local(factor, panel_inverse, sim_maps, harmonics):
        _, rows, maps = sim_maps.shape
        cols = panel_inverse.shape[2]
        part = rows // n_col
        fits = (
            rows % n_col == 0
            and part % SUBLANES == 0
            and cols % part == 0
            and cols % LANES == 0
            and maps % LANES == 0
            and maps // n_row % SUBLANES == 0
            and rows % cols == 0
            and n_col % 2 == 0
            and n_col >= 4
            and n_col <= 8
            and sim_maps.shape[0] > 2
        )
        if not fits:
            return plain(factor, panel_inverse, sim_maps, harmonics)
        return fused(n_row, n_col, factor, panel_inverse, sim_maps, harmonics)

    in_specs = (P(None, "row", "col"), P(None, "row", "col"), P(None, "row", None), P("col", "row"))
    out_specs = (P(None, "row", None), P("row", "col"))
    return jax.shard_map(local, mesh=mesh, in_specs=in_specs, out_specs=out_specs, check_vma=False)
```

```python
import functools

import jax
import jax.numpy as jnp
from jax import lax
from jax.experimental import pallas as pl
from jax.experimental.pallas import tpu as pltpu
from jax.sharding import PartitionSpec as P

MESH = pl.DeviceIdType.MESH
CHUNK = 896
LANES = 128
SUBLANES = 8


def split(value):
    high = value.astype(jnp.bfloat16)
    low = (value - high.astype(jnp.float32)).astype(jnp.bfloat16)
    return high, low


def dot3(mat_high, mat_low, value):
    high, low = split(value)
    mul = functools.partial(jnp.dot, preferred_element_type=jnp.float32)
    return mul(mat_high, high) + (mul(mat_high, low) + mul(mat_low, high))


def kernel(
    n_row, n_col, factor_hbm, inv_hbm, sim_hbm, harm_hbm, solved_ref, proj_ref,
    factor, inv, sim, harm, f_high, f_low, i_high, i_low,
    partial, gathered, piece, xbuf, xint, ibuf, fcol, fbuf, g_high, g_low, sol, stacked, outs, up, down,
    load_sem, rs_send, rs_recv, bc_send, bc_recv, im_send, im_recv, ia_send, ia_recv, fz_send, fz_recv,
    ag_send, ag_recv, pj_send, up_sem, down_sem,
):
    panels, rows, maps = sim.shape
    cols = inv.shape[2]
    part = rows // n_col
    out_rows = maps // n_row
    stages = 2 * panels - 1
    modes = harm.shape[0]
    chunks = outs.shape[0]
    r, c = lax.axis_index("row"), lax.axis_index("col")
    me = r * n_col + c
    total = n_row * n_col

    loads = [
        pltpu.make_async_copy(src, dst, load_sem.at[i])
        for i, (src, dst) in enumerate(
            ((sim_hbm, sim), (inv_hbm, inv), (factor_hbm, factor), (harm_hbm, harm))
        )
    ]
    for load in loads:
        load.start()

    barrier = pltpu.get_barrier_semaphore()

    def greet(d, carry):
        peer = (me + d) % total
        pl.semaphore_signal(
            barrier, inc=1, device_id=(peer // n_col, peer % n_col), device_id_type=MESH
        )
        return carry

    lax.fori_loop(1, total, greet, 0)
    xint[...] = jnp.zeros_like(xint)
    loads[0].wait()
    loads[1].wait()
    for k in range(panels):
        i_high[k], i_low[k] = split(inv[k])
    pl.semaphore_wait(barrier, total - 1)

    mine = pl.ds(pl.multiple_of(c * part, part), part)
    owner = (r * rows + c * part) // cols
    inside = (r * rows + c * part) % cols
    place = pl.ds(pl.multiple_of(inside, part), part)
    pieces = cols // part

    def spread(stage, source):
        def one(d, carry):
            pltpu.make_async_remote_copy(
                src_ref=source,
                dst_ref=xbuf.at[stage, place],
                send_sem=bc_send.at[stage],
                recv_sem=bc_recv.at[stage],
                device_id=((r + d) % n_row, owner),
                device_id_type=MESH,
            ).start()
            return carry

        @pl.when(owner != c)
        def _():
            one(0, 0)

        @pl.when(owner == c)
        def _():
            xbuf[stage, place] = source[...]

        lax.fori_loop(1, n_row, one, 0)

    def drain(sem, ref):
        pltpu.make_async_copy(ref, ref, sem).wait()

    def take(stage):
        @pl.when(owner != c)
        def _():
            drain(bc_recv.at[stage], xbuf.at[stage])

        @pl.when(owner == c)
        def _():
            drain(bc_recv.at[stage], xbuf.at[stage, pl.ds(0, (pieces - 1) * part)])

    def reduce(stage, value):
        partial[stage] = value

        def one(d, carry):
            peer = (c + d) % n_col
            pltpu.make_async_remote_copy(
                src_ref=partial.at[stage, pl.ds(pl.multiple_of(peer * part, part), part)],
                dst_ref=gathered.at[stage, d - 1],
                send_sem=rs_send.at[stage],
                recv_sem=rs_recv.at[stage],
                device_id=(r, peer),
                device_id_type=MESH,
            ).start()
            return carry

        lax.fori_loop(1, n_col, one, 0)
        return

    def reduced(stage):
        drain(rs_recv.at[stage], gathered.at[stage])
        total_value = partial[stage, mine]
        for d in range(n_col - 1):
            total_value = total_value + gathered[stage, d]
        return total_value

    def share(k, source):
        def one(d, carry):
            pltpu.make_async_remote_copy(
                src_ref=source,
                dst_ref=sol.at[k, mine],
                send_sem=ag_send.at[k],
                recv_sem=ag_recv.at[k],
                device_id=(r, (c + d) % n_col),
                device_id_type=MESH,
            ).start()
            return carry

        lax.fori_loop(1, n_col, one, 0)
        sol[k, mine] = source[...]

    mate = c + 1 - 2 * (c % 2)

    def own_block(g):
        ibuf[g, c] = inv[g + 2]
        pltpu.make_async_remote_copy(
            src_ref=inv.at[g + 2], dst_ref=ibuf.at[g, c],
            send_sem=im_send.at[g, 0], recv_sem=im_recv.at[g],
            device_id=(r, mate), device_id_type=MESH,
        ).start()

    def across(g, d):
        pltpu.make_async_remote_copy(
            src_ref=inv.at[g + 2], dst_ref=ibuf.at[g, c],
            send_sem=ia_send.at[g, d - 1], recv_sem=ia_recv.at[g, d - 1],
            device_id=(r, (c + 2 * d) % n_col), device_id_type=MESH,
        ).start()

    def relay(g, d):
        source = (c + n_col - 2 * d) % n_col
        drain(ia_recv.at[g, d - 1], ibuf.at[g, source])
        pltpu.make_async_remote_copy(
            src_ref=ibuf.at[g, source], dst_ref=ibuf.at[g, source],
            send_sem=im_send.at[g, d], recv_sem=im_recv.at[g],
            device_id=(r, mate), device_id_type=MESH,
        ).start()

    def along(g, d):
        pltpu.make_async_remote_copy(
            src_ref=fcol.at[g], dst_ref=fbuf.at[g, r],
            send_sem=fz_send.at[g], recv_sem=fz_recv.at[g],
            device_id=((r + d) % n_row, c), device_id_type=MESH,
        ).start()

    def pick(g):
        wide, narrow = cols * panels, cols
        at = lax.broadcasted_iota(jnp.int32, (wide, narrow), 0)
        to = lax.broadcasted_iota(jnp.int32, (wide, narrow), 1)
        chosen = jnp.where(at == to * panels + (g + 1), 1.0, 0.0).astype(jnp.bfloat16)
        mul = functools.partial(jnp.dot, preferred_element_type=jnp.float32)
        fcol[g] = mul(f_high[g + 1], chosen) + mul(f_low[g + 1], chosen)
        fbuf[g, r] = fcol[g]

    def product(g):
        drain(im_recv.at[g], ibuf.at[g, pl.ds(0, n_col // 2)])
        drain(fz_recv.at[g], fbuf.at[g, pl.ds(0, n_row - 1)])
        value = jnp.zeros((rows, cols), jnp.float32)
        per = rows // cols
        for q in range(n_col):
            high, low = split(ibuf[g, q])
            value = value + dot3(high, low, fbuf[g, q // per, (q % per) * cols : (q % per + 1) * cols])
        g_high[g], g_low[g] = split(value)

    half = n_col // 2
    plan = {}
    for g in range(panels - 2):
        at = 1 + 3 * g
        tasks = [(0, own_block, (g,))]
        tasks += [(d - 1, across, (g, d)) for d in range(1, half)]
        tasks += [(min(d - 1, 2), along, (g, d)) for d in range(1, n_row)]
        tasks += [(3, relay, (g, d)) for d in range(1, half)]
        tasks += [(4, product, (g,))]
        for offset, task, arguments in tasks:
            plan.setdefault(at + offset, []).append((task, arguments))

    def aside(point):
        for task, arguments in plan.pop(point, ()):
            task(*arguments)

    def extra(k):
        return panels + k - 1

    rest = pl.ds(0, rows - part)

    def gather(k):
        drain(ag_recv.at[k], sol.at[k, rest])
        value = sol[k]
        solved_ref[k] = value
        stacked[pl.ds(k, rows, stride=panels), :] = value

    spread(0, sim.at[0, mine])
    loads[2].wait()
    for j in range(1, panels):
        f_high[j - 1], f_low[j - 1] = split(factor[j])
    for g in range(panels - 2):
        pick(g)
    take(0)
    reduce(0, dot3(i_high[0], i_low[0], xbuf[0]))
    aside(1)
    piece[0] = reduced(0)
    spread(1, piece.at[0])
    aside(2)
    share(0, piece.at[0])
    take(1)
    xint[pl.ds(0, cols, stride=panels), :] = xbuf[1]
    reduce(1, dot3(f_high[0], f_low[0], xint[...]))
    if panels > 2:
        reduce(extra(2), dot3(f_high[1], f_low[1], xint[...]))
    aside(3)
    piece[1] = sim[1, mine] - reduced(1)
    spread(2, piece.at[1])
    if panels > 2:
        piece[extra(2)] = sim[2, mine] - reduced(extra(2))
        spread(extra(2), piece.at[extra(2)])
    aside(4)
    take(2)
    reduce(2, dot3(i_high[1], i_low[1], xbuf[2]))
    aside(5)
    piece[2] = reduced(2)
    point = 6
    for k in range(2, panels):
        slot = k + 1
        spread(slot, piece.at[slot - 1])
        if k > 2:
            piece[extra(k)] = sim[k, mine] - reduced(extra(k))
            spread(extra(k), piece.at[extra(k)])
        share(k - 1, piece.at[slot - 1])
        aside(point)
        take(extra(k))
        ahead = dot3(i_high[k], i_low[k], xbuf[extra(k)])
        take(slot)
        reduce(slot, ahead - dot3(g_high[k - 2], g_low[k - 2], xbuf[slot]))
        if k + 1 < panels:
            xint[pl.ds(k - 1, cols, stride=panels), :] = xbuf[slot]
            reduce(extra(k + 1), dot3(f_high[k], f_low[k], xint[...]))
        aside(point + 1)
        if k == panels - 1:
            loads[3].wait()
            for done in range(k):
                gather(done)
        piece[slot] = reduced(slot)
        point = point + 2
    share(panels - 1, piece.at[panels])
    assert not plan

    gather(panels - 1)
    turned = jnp.transpose(stacked[...], (1, 0)).astype(jnp.bfloat16)

    def forward(i, p, step, slots, sems):
        block = pl.ds(p * out_rows, out_rows)

        @pl.when((r - step >= 0) & (r - step < n_row))
        def _():
            drain(sems.at[i, p], slots.at[i, p])
            outs[i, block] = outs[i, block] + slots[i, p]

        pltpu.make_async_remote_copy(
            src_ref=outs.at[i, block],
            dst_ref=slots.at[i, p],
            send_sem=pj_send.at[i, p],
            recv_sem=sems.at[i, p],
            device_id=(r + step, c),
            device_id_type=MESH,
        ).start()

    own = pl.ds(pl.multiple_of(r * out_rows, out_rows), out_rows)
    for i in range(chunks + n_row - 1):
        if i < chunks:
            size = min(CHUNK, modes - i * CHUNK)
            outs[i, :, :size] = lax.dot_general(
                turned, harm[i * CHUNK : i * CHUNK + size, :],
                (((1,), (1,)), ((), ())), preferred_element_type=jnp.float32,
            )
        for step, lag, slots, sems in ((1, r, up, up_sem), (-1, n_row - 1 - r, down, down_sem)):
            at = i - lag
            for p in range(n_row):
                target = n_row - 1 - p if step == 1 else p

                @pl.when(((target - r) * step > 0) & (at >= 0) & (at < chunks))
                def _():
                    forward(at, target, step, slots, sems)

    for i in range(chunks):
        size = min(CHUNK, modes - i * CHUNK)

        @pl.when(r > 0)
        def _():
            drain(up_sem.at[i, r], up.at[i, r])
            outs[i, own] = outs[i, own] + up[i, r]

        @pl.when(r < n_row - 1)
        def _():
            drain(down_sem.at[i, r], down.at[i, r])
            outs[i, own] = outs[i, own] + down[i, r]

        proj_ref[:, i * CHUNK : i * CHUNK + size] = outs[i, own][:, :size]

    for stage in range(stages):
        drain(rs_send.at[stage], gathered.at[stage])

        @pl.when(owner != c)
        def _():
            drain(bc_send.at[stage], sol.at[0, pl.ds(0, n_row * part)])

        @pl.when(owner == c)
        def _():
            drain(bc_send.at[stage], sol.at[0, pl.ds(0, (n_row - 1) * part)])

    for g in range(panels - 2):
        for d in range(half):
            drain(im_send.at[g, d], ibuf.at[g, d])
        for d in range(half - 1):
            drain(ia_send.at[g, d], ibuf.at[g, d])
        drain(fz_send.at[g], fbuf.at[g, pl.ds(0, n_row - 1)])
    for k in range(panels):
        drain(ag_send.at[k], sol.at[k, rest])

    for i in range(chunks):
        for p in range(n_row):
            @pl.when(r != p)
            def _():
                drain(pj_send.at[i, p], up.at[i, p])


def fused(n_row, n_col, factor, inv, sim, harm):
    panels, rows, maps = sim.shape
    cols = inv.shape[2]
    modes = harm.shape[0]
    part = rows // n_col
    stages = 2 * panels - 1
    chunks = -(-modes // CHUNK)
    f32, bf16 = jnp.float32, jnp.bfloat16
    any_space = pl.BlockSpec(memory_space=pl.ANY)
    vmem = pl.BlockSpec(memory_space=pltpu.VMEM)
    dma = pltpu.SemaphoreType.DMA
    return pl.pallas_call(
        functools.partial(kernel, n_row, n_col),
        out_shape=(
            jax.ShapeDtypeStruct(sim.shape, f32),
            jax.ShapeDtypeStruct((maps // n_row, modes), f32),
        ),
        in_specs=[any_space] * 4,
        out_specs=(vmem, vmem),
        scratch_shapes=[
            pltpu.VMEM(factor.shape, f32),
            pltpu.VMEM(inv.shape, f32),
            pltpu.VMEM(sim.shape, f32),
            pltpu.VMEM(harm.shape, bf16),
            pltpu.VMEM((panels - 1,) + factor.shape[1:], bf16),
            pltpu.VMEM((panels - 1,) + factor.shape[1:], bf16),
            pltpu.VMEM(inv.shape, bf16),
            pltpu.VMEM(inv.shape, bf16),
            pltpu.VMEM((stages, rows, maps), f32),
            pltpu.VMEM((stages, n_col - 1, part, maps), f32),
            pltpu.VMEM((stages, part, maps), f32),
            pltpu.VMEM((stages, cols, maps), f32),
            pltpu.VMEM((cols * panels, maps), f32),
            pltpu.VMEM((panels - 2, n_col, rows, cols), f32),
            pltpu.VMEM((panels - 2, rows, cols), f32),
            pltpu.VMEM((panels - 2, n_row, rows, cols), f32),
            pltpu.VMEM((panels - 2, rows, cols), bf16),
            pltpu.VMEM((panels - 2, rows, cols), bf16),
            pltpu.VMEM(sim.shape, f32),
            pltpu.VMEM((rows * panels, maps), f32),
            pltpu.VMEM((chunks, maps, CHUNK), f32),
            pltpu.VMEM((chunks, n_row, maps // n_row, CHUNK), f32),
            pltpu.VMEM((chunks, n_row, maps // n_row, CHUNK), f32),
            dma((4,)),
            dma((stages,)), dma((stages,)), dma((stages,)), dma((stages,)),
            dma((panels - 2, n_col // 2)), dma((panels - 2,)),
            dma((panels - 2, n_col // 2 - 1)), dma((panels - 2, n_col // 2 - 1)),
            dma((panels - 2,)), dma((panels - 2,)),
            dma((panels,)), dma((panels,)),
            dma((chunks, n_row)), dma((chunks, n_row)), dma((chunks, n_row)),
        ],
        compiler_params=pltpu.CompilerParams(
            collective_id=0, has_side_effects=True, vmem_limit_bytes=62 * 1024 * 1024
        ),
    )(factor, inv, sim, harm)


def plain(factor, panel_inverse, sim_maps, harmonics):
    panels = factor.shape[0]
    row_count = factor.shape[1]
    col_count = factor.shape[2] // panels
    map_count = sim_maps.shape[2]
    col_index = lax.axis_index("col")
    columns = jnp.zeros((col_count, panels, map_count), jnp.float32)
    results = []
    for panel in range(panels):
        flat_cols = columns.reshape(col_count * panels, map_count)
        partial_value = jnp.dot(
            factor[panel], flat_cols,
            precision=lax.Precision.HIGHEST, preferred_element_type=jnp.float32,
        )
        update = lax.psum(partial_value, "col")
        rhs_now = sim_maps[panel] - update
        whole = lax.all_gather(rhs_now, "row", axis=0, tiled=True)
        piece = lax.dynamic_slice_in_dim(whole, col_index * col_count, col_count, 0)
        partial_inv = jnp.dot(
            panel_inverse[panel], piece,
            precision=lax.Precision.HIGHEST, preferred_element_type=jnp.float32,
        )
        result = lax.psum(partial_inv, "col")
        whole_solved = lax.all_gather(result, "row", axis=0, tiled=True)
        solved_piece = lax.dynamic_slice_in_dim(whole_solved, col_index * col_count, col_count, 0)
        columns = columns.at[:, panel, :].set(solved_piece)
        results.append(result)
    solved = jnp.stack(results)
    solved_low = solved.astype(jnp.bfloat16)
    stacked = jnp.transpose(solved_low, (1, 0, 2)).reshape(row_count * panels, map_count)
    projected = lax.psum_scatter(
        lax.dot_general(
            stacked, harmonics, (((0,), (1,)), ((), ())), preferred_element_type=jnp.float32
        ),
        "row", scatter_dimension=0, tiled=True,
    )
    return (solved, projected)


def solution(mesh):
    n_row, n_col = mesh.shape["row"], mesh.shape["col"]

    def local(factor, panel_inverse, sim_maps, harmonics):
        _, rows, maps = sim_maps.shape
        cols = panel_inverse.shape[2]
        part = rows // n_col
        fits = (
            rows % n_col == 0
            and part % SUBLANES == 0
            and cols % part == 0
            and cols % LANES == 0
            and maps % LANES == 0
            and maps // n_row % SUBLANES == 0
            and rows % cols == 0
            and n_col % 2 == 0
            and n_col >= 4
            and n_col <= 8
            and sim_maps.shape[0] > 2
        )
        if not fits:
            return plain(factor, panel_inverse, sim_maps, harmonics)
        return fused(n_row, n_col, factor, panel_inverse, sim_maps, harmonics)

    in_specs = (P(None, "row", "col"), P(None, "row", "col"), P(None, "row", None), P("col", "row"))
    out_specs = (P(None, "row", None), P("row", "col"))
    return jax.shard_map(local, mesh=mesh, in_specs=in_specs, out_specs=out_specs, check_vma=False)
```
